32 devices in a mesh: gx: 4 (over z), gy: 8 (over y, x, core).
Axes of the slice: x: 2, y: 2, z: 4, core: 2. Of those that a mesh axis runs over, the one named last changes fastest.
Arguments:
- source: float32 [128, 256, 128], P('gx', 'gy'), may hold values from -6 to 6
- inverse_density: float32 [128, 256, 128], P('gx', 'gy'), may hold values from 1 to 7
Outputs:
- correction: float32 [128, 256, 128], P('gx', 'gy')
The draws below stay inside these ranges and needn't reach their ends.
All inputs are finite; a program needn't handle non-finite values.
Results may differ from the reference program's by a relative error of at most 0.0001.
Values sent between devices are 32-bit elements; how exact they have to be, the bound alone decides.
A program may use at most 128 MiB of HBM per device.

```python
import math
import jax
import jax.numpy as jnp

NZ = 128
LEVELS = 4
NU1 = 3
NU2 = 2
NC = 5
NX = 128
NY = 256


def draw_source(key, part):
    extent = (NX, NY, NZ)
    return jnp.clip(jax.random.normal(key, extent, jnp.float32), -6.0, 6.0)


def block_scale(key, dims, split, smallest, top_value):
    def one(dim, parts):
        steps = jax.random.uniform(jax.random.fold_in(jax.random.fold_in(key, 6), dim), (parts,), jnp.float32, smallest / len(split), top_value / len(split))
        return jnp.repeat(jnp.exp(steps), dims[dim] // parts).reshape((-1,) + (1,) * (len(dims) - dim - 1))

    level = one(*split[0])
    for cut in split[1:]:
        level = level * one(*cut)
    return level


def setup_inputs(seed: int = 0) -> dict:
    key_list = jax.random.split(jax.random.key(seed), 3)
    return {
        "source": draw_source(jax.random.fold_in(key_list[2], 71), 0),
        "inverse_density": jnp.clip(jnp.exp(math.log(7.0) - 1.9459101 * jax.random.uniform(key_list[1], (NX, NY, NZ), jnp.float32) ** block_scale(key_list[1], (NX, NY, NZ), ((0, 4), (1, 8)), -0.2, 0.2)), 1.0, 7.0),
    }


OMEGA = 0.8


def harmonic(left_value, right_value):
    return 2.0 * left_value * right_value / (left_value + right_value)


def centre_and_others(padded):
    centre = padded[1:-1, 1:-1, 1:-1]
    others = [padded[:-2, 1:-1, 1:-1], padded[2:, 1:-1, 1:-1], padded[1:-1, :-2, 1:-1],
              padded[1:-1, 2:, 1:-1], padded[1:-1, 1:-1, :-2], padded[1:-1, 1:-1, 2:]]
    return centre, others


def coefficients(coef_padded, factor):
    centre, others = centre_and_others(coef_padded)
    couplings = [factor * harmonic(centre, neighbour) for neighbour in others]
    diagonal = couplings[0] + couplings[1] + couplings[2] + couplings[3] + couplings[4] + couplings[5]
    return couplings, diagonal


def residual_of(field_padded, source, couplings):
    centre, others = centre_and_others(field_padded)
    applied = couplings[0] * (centre - others[0])
    for position in range(1, 6):
        applied = applied + couplings[position] * (centre - others[position])
    return source - applied


def pad_depth(values, replicate_ends):
    if replicate_ends:
        return jnp.concatenate([values[:, :, :1], values, values[:, :, -1:]], axis=2)
    zero_layer = jnp.zeros(values.shape[:2] + (1,), jnp.float32)
    return jnp.concatenate([zero_layer, values, zero_layer], axis=2)


def wrap_rims(values, replicate_ends):
    widened = jnp.pad(values, ((1, 1), (1, 1), (0, 0)), mode="wrap")
    return pad_depth(widened, replicate_ends)


def restrict(values):
    extent = values.shape
    return jnp.mean(values.reshape(extent[0] // 2, 2, extent[1] // 2, 2, extent[2] // 2, 2), axis=(1, 3, 5))


def prolong(values):
    return jnp.repeat(jnp.repeat(jnp.repeat(values, 2, axis=0), 2, axis=1), 2, axis=2)


def reference(source, inverse_density):
    records = []
    current_source, current_beta = source, inverse_density
    for level_number in range(LEVELS):
        factor = 0.25 ** level_number
        couplings, diagonal = coefficients(wrap_rims(current_beta, True), factor)
        sweeps = NC if level_number == LEVELS - 1 else NU1
        iterate = OMEGA * current_source / diagonal
        for sweep_number in range(sweeps - 1):
            iterate = iterate + OMEGA * residual_of(wrap_rims(iterate, False), current_source, couplings) / diagonal
        records.append((iterate, current_source, couplings, diagonal))
        if level_number < LEVELS - 1:
            residual = residual_of(wrap_rims(iterate, False), current_source, couplings)
            current_source = restrict(residual)
            current_beta = restrict(current_beta)
    correction = records[LEVELS - 1][0]
    for level_number in range(LEVELS - 2, -1, -1):
        iterate, level_source, couplings, diagonal = records[level_number]
        iterate = iterate + prolong(correction)
        for sweep_number in range(NU2):
            iterate = iterate + OMEGA * residual_of(wrap_rims(iterate, False), level_source, couplings) / diagonal
        correction = iterate
    return correction
```

```python
import functools

import jax
import jax.numpy as jnp
from jax import lax
from jax.experimental import pallas as pl
from jax.experimental.pallas import tpu as pltpu
from jax.sharding import PartitionSpec as P

MESH = pl.DeviceIdType.MESH
OMEGA = 0.8
F32 = jnp.float32

PLANES = (42, 28, 40, 20)
ROWS = (48, 32, 40, 24)
X_AT = (5, 6, 16, 8)
Y_AT = (8, 8, 16, 8)
OWN = 32
NEAR = [(dx, dy) for dx in (1, -1, 0) for dy in (0, 1, -1) if (dx, dy) != (0, 0)]


def far_offsets(peers):
    return (-1, 0, 1, 2) if peers == 4 else (-2, -1, 0, 1, 2)


def far_slot(peers, offset):
    return (offset + 2) % 4 if peers == 4 else offset + 2


def lanes(value, shift):
    return pltpu.roll(value, shift % 128, 1)


def rows(value, shift):
    return pltpu.roll(value, shift % value.shape[0], 0)


def lane_index(height):
    return lax.broadcasted_iota(jnp.int32, (height, 128), 1)


def swap_lanes(value, step):
    low = (lane_index(value.shape[0]) & step) == 0
    return jnp.where(low, lanes(value, -step), lanes(value, step))


def loop(first, last, body, unroll=2):
    count = last - first
    whole = count // unroll

    def step(trip, carry):
        for inner in range(unroll):
            body(first + trip * unroll + inner)
        return carry

    lax.fori_loop(0, whole, step, 0)
    for index in range(first + whole * unroll, last):
        body(index)


def build(level, b, f, cx, cy, cz, diag, gain, u):
    height = ROWS[level]
    factor2 = 2.0 * 0.25**level
    step = 2**level
    lane = lane_index(height)
    top = lane >= 128 - step
    ends = top | (lane < step)

    def pair(left, right):
        return factor2 * left * right / (left + right)

    def one(x, carry):
        before, here = carry
        after = b[x + 1]
        c_x = pair(here, after)
        c_y = pair(here, rows(here, -1))
        c_z = jnp.where(top, 0.0, pair(here, lanes(here, -step)))
        total = before + c_x + c_y + rows(c_y, 1) + c_z + lanes(c_z, step)
        total = total + jnp.where(ends, (0.5 * factor2) * here, 0.0)
        scaled = OMEGA / total
        cx[x] = c_x
        cy[x] = c_y
        cz[x] = c_z
        diag[x] = total
        gain[x] = scaled
        u[x] = scaled * f[x]
        return (c_x, after)

    first = pair(b[0], b[1])
    cx[0] = first

    def two(trip, carry):
        carry = one(1 + 2 * trip, carry)
        return one(2 + 2 * trip, carry)

    lax.fori_loop(0, (PLANES[level] - 2) // 2, two, (first, b[1]))


def spread(level, x, u, cx, cy, cz, span):
    here = u[x, span]
    along_y = cy[x, span]
    along_z = cz[x, span]
    step = 2**level
    total = cx[x, span] * u[x + 1, span] + cx[x - 1, span] * u[x - 1, span]
    total = total + (along_y * rows(here, -1) + rows(along_y * here, 1))
    total = total + (along_z * lanes(here, -step) + lanes(along_z * here, step))
    return here, total


def sweep(level, first, last, source, target, f, cx, cy, cz, gain, span=None):
    span = pl.ds(0, ROWS[level]) if span is None else span

    def one(x):
        here, total = spread(level, x, source, cx, cy, cz, span)
        target[x, span] = (1.0 - OMEGA) * here + gain[x, span] * (f[x, span] + total)

    loop(first, last, one)


def pair_mean(level, tmp, slot, value, count):
    tmp[slot, pl.ds(0, 2 * count)] = value
    summed = tmp[slot, pl.ds(0, count, stride=2)] + tmp[slot, pl.ds(1, count, stride=2)]
    return 0.125 * (summed + swap_lanes(summed, 2**level))


def restrict_field(level, b, target, tmp, fine_x, planes, fine_row, count, at_x, at_row):
    span = pl.ds(fine_row, 2 * count)

    def one(i):
        value = b[fine_x + 2 * i, span] + b[fine_x + 2 * i + 1, span]
        target[at_x + i, pl.ds(at_row, count)] = pair_mean(level, tmp, i, value, count)

    loop(0, planes, one)


def restrict_residual(level, u, f, cx, cy, cz, diag, target, tmp, fine_x, planes, fine_row, count, at_x, at_row):
    span = pl.ds(0, ROWS[level])

    def left(x):
        here, total = spread(level, x, u, cx, cy, cz, span)
        return f[x] + total - diag[x] * here

    def one(i):
        value = (left(fine_x + 2 * i) + left(fine_x + 2 * i + 1))[fine_row : fine_row + 2 * count]
        target[at_x + i, pl.ds(at_row, count)] = pair_mean(level, tmp, i, value, count)

    loop(0, planes, one, 1)


def add_coarse(u, coarse, tmp, first, planes, coarse_x, coarse_row, fine_row, count):
    def one(i):
        value = coarse[coarse_x + i, pl.ds(coarse_row, count)]
        tmp[i, pl.ds(0, count, stride=2)] = value
        tmp[i, pl.ds(1, count, stride=2)] = value
        both = tmp[i, pl.ds(0, 2 * count)]
        span = pl.ds(fine_row, 2 * count)
        u[first + 2 * i, span] = u[first + 2 * i, span] + both
        u[first + 2 * i + 1, span] = u[first + 2 * i + 1, span] + both

    loop(0, planes, one)


def pack_1(wide, packed):
    even = (lane_index(16) & 1) == 0
    span = pl.ds(8, 16)

    def one(i):
        packed[3 + i, span] = jnp.where(even, wide[6 + 2 * i, span], wide[7 + 2 * i, span])

    loop(0, 8, one)


def unpack_1(packed, wide):
    even = (lane_index(32) & 1) == 0

    def one(i):
        value = packed[i]
        other = swap_lanes(value, 1)
        wide[2 * i] = jnp.where(even, value, other)
        wide[2 * i + 1] = jnp.where(even, other, value)

    loop(0, 14, one)


def pack_2(wide, packed, slot):
    lane = lane_index(8)
    span = pl.ds(16, 8)
    for p in range(2):
        at = 16 + 4 * p
        low = jnp.where((lane & 1) == 0, wide[at, span], wide[at + 1, span])
        high = jnp.where((lane & 1) == 0, wide[at + 2, span], wide[at + 3, span])
        packed[slot, p] = jnp.where((lane & 2) == 0, low, high)


def unpack_2(nx, ny, packed, wide):
    lane = lane_index(8)
    even = (lane & 1) == 0
    low = (lane & 2) == 0

    def one(trip, carry):
        block = trip // 2
        part = trip % 2
        slot_x = block % 4 if nx == 4 else block
        for j in range(5):
            slot = slot_x * 5 + far_slot(ny, j - 2)
            value = packed[slot, part]
            other = swap_lanes(value, 2)
            span = pl.ds(8 * j, 8)
            for half, kept in enumerate((jnp.where(low, value, other), jnp.where(low, other, value))):
                swapped = swap_lanes(kept, 1)
                wide[4 * trip + 2 * half, span] = jnp.where(even, kept, swapped)
                wide[4 * trip + 2 * half + 1, span] = jnp.where(even, swapped, kept)
        return carry

    lax.fori_loop(0, 10, one, 0)


def side(offset, length, width, at):
    if offset == 0:
        return pl.ds(0, length), pl.ds(at, length)
    if offset == 1:
        return pl.ds(length - width, width), pl.ds(at - width, width)
    return pl.ds(0, width), pl.ds(at + length, width)


def kernel(nx, ny, f_in, b_in, out, *refs):
    fields = [refs[9 * level : 9 * level + 9] for level in range(4)]
    tmp, pf1, pb1, pf2, pb2, load_sem, send_sem, recv_sem = refs[36:]
    (b0, f0, u0, v0, cx0, cy0, cz0, d0, g0) = fields[0]
    (b1, f1, u1, v1, cx1, cy1, cz1, d1, g1) = fields[1]
    (b2, f2, u2, v2, cx2, cy2, cz2, d2, g2) = fields[2]
    (b3, f3, u3, v3, cx3, cy3, cz3, d3, g3) = fields[3]
    mx, my = lax.axis_index("gx"), lax.axis_index("gy")
    far = [(dx, dy) for dx in far_offsets(nx) for dy in far_offsets(ny) if (dx, dy) != (0, 0)]

    def peer(dx, dy):
        return (lax.rem(mx + dx + nx, nx), lax.rem(my + dy + ny, ny))

    barrier = pltpu.get_barrier_semaphore()
    greet = sorted(set(far) | set((-dx, -dy) for dx, dy in far))
    for dx, dy in greet:
        pl.semaphore_signal(barrier, inc=1, device_id=peer(dx, dy), device_id_type=MESH)

    inside = (pl.ds(5, OWN), pl.ds(8, OWN))
    load_b = pltpu.make_async_copy(b_in, b0.at[inside], load_sem.at[0])
    load_f = pltpu.make_async_copy(f_in, f0.at[inside], load_sem.at[1])
    load_b.start()
    load_f.start()
    pl.semaphore_wait(barrier, len(greet))

    started = []

    def send(source, target, dx, dy):
        number = len(started)
        copy = pltpu.make_async_remote_copy(
            src_ref=source,
            dst_ref=target,
            send_sem=send_sem.at[number],
            recv_sem=recv_sem.at[number],
            device_id=peer(dx, dy),
            device_id_type=MESH,
        )
        copy.start()
        started.append(copy)
        return copy

    fine = []
    for dx, dy in NEAR:
        for source, target, width in ((b_in, b0, 5), (f_in, f0, 4)):
            from_x, to_x = side(dx, OWN, width - (dy != 0), 5)
            from_y, to_y = side(dy, OWN, 8, 8)
            fine.append(send(source.at[from_x, from_y], target.at[to_x, to_y], dx, dy))

    def send_1(packed):
        copies = []
        for dx, dy in NEAR:
            from_x, to_x = side(dx, 8, 3, 3)
            from_y, to_y = side(dy, 16, 8, 8)
            from_x = pl.ds(from_x.start + 3, from_x.size)
            from_y = pl.ds(from_y.start + 8, from_y.size)
            copies.append(send(packed.at[from_x, from_y], packed.at[to_x, to_y], dx, dy))
        return copies

    def slot_2(dx, dy):
        return far_slot(nx, dx) * 5 + far_slot(ny, dy)

    def send_2(packed):
        return [send(packed.at[slot_2(0, 0)], packed.at[slot_2(-dx, -dy)], dx, dy) for dx, dy in far]

    load_b.wait()
    restrict_field(0, b0, b1, tmp, 5, 16, 8, 16, 6, 8)
    pack_1(b1, pb1)
    middle_b = send_1(pb1)
    restrict_field(1, b1, b2, tmp, 6, 8, 8, 8, 16, 16)
    pack_2(b2, pb2, slot_2(0, 0))
    coarse_b = send_2(pb2)
    load_f.wait()
    for copy in fine:
        copy.wait_recv()

    build(0, b0, f0, cx0, cy0, cz0, d0, g0, u0)
    sweep(0, 2, 40, u0, v0, f0, cx0, cy0, cz0, g0)
    sweep(0, 3, 39, v0, u0, f0, cx0, cy0, cz0, g0)
    restrict_residual(0, u0, f0, cx0, cy0, cz0, d0, f1, tmp, 5, 16, 8, 16, 6, 8)
    pack_1(f1, pf1)
    middle_f = send_1(pf1)
    for copy in middle_b:
        copy.wait_recv()
    unpack_1(pb1, b1)
    for copy in middle_f:
        copy.wait_recv()
    unpack_1(pf1, f1)

    build(1, b1, f1, cx1, cy1, cz1, d1, g1, u1)
    sweep(1, 2, 26, u1, v1, f1, cx1, cy1, cz1, g1)
    sweep(1, 3, 25, v1, u1, f1, cx1, cy1, cz1, g1)
    restrict_residual(1, u1, f1, cx1, cy1, cz1, d1, f2, tmp, 6, 8, 8, 8, 16, 16)
    pack_2(f2, pf2, slot_2(0, 0))
    coarse_f = send_2(pf2)
    for copy in coarse_b:
        copy.wait_recv()
    unpack_2(nx, ny, pb2, b2)
    restrict_field(2, b2, b3, tmp, 0, 20, 0, 20, 0, 0)
    for copy in coarse_f:
        copy.wait_recv()
    unpack_2(nx, ny, pf2, f2)

    build(2, b2, f2, cx2, cy2, cz2, d2, g2, u2)
    sweep(2, 2, 38, u2, v2, f2, cx2, cy2, cz2, g2)
    sweep(2, 3, 37, v2, u2, f2, cx2, cy2, cz2, g2)
    restrict_residual(2, u2, f2, cx2, cy2, cz2, d2, f3, tmp, 4, 16, 0, 20, 2, 0)

    build(3, b3, f3, cx3, cy3, cz3, d3, g3, u3)
    sweep(3, 3, 17, u3, v3, f3, cx3, cy3, cz3, g3)
    sweep(3, 4, 16, v3, u3, f3, cx3, cy3, cz3, g3)
    sweep(3, 5, 15, u3, v3, f3, cx3, cy3, cz3, g3)
    sweep(3, 6, 14, v3, u3, f3, cx3, cy3, cz3, g3)

    add_coarse(u2, u3, tmp, 12, 8, 6, 4, 8, 12)
    middle = pl.ds(8, 24)
    sweep(2, 13, 27, u2, v2, f2, cx2, cy2, cz2, g2, middle)
    sweep(2, 14, 26, v2, u2, f2, cx2, cy2, cz2, g2, middle)

    add_coarse(u1, u2, tmp, 2, 12, 14, 12, 0, 16)
    sweep(1, 4, 24, u1, v1, f1, cx1, cy1, cz1, g1)
    sweep(1, 5, 23, v1, u1, f1, cx1, cy1, cz1, g1)

    add_coarse(u0, u1, tmp, 3, 18, 5, 4, 0, 24)
    sweep(0, 4, 38, u0, v0, f0, cx0, cy0, cz0, g0)

    whole = pl.ds(0, ROWS[0])

    def last(x):
        here, total = spread(0, x, v0, cx0, cy0, cz0, whole)
        value = (1.0 - OMEGA) * here + g0[x] * (f0[x] + total)
        out[x - 5] = value[8:40]

    loop(5, 37, last)
    for copy in started:
        copy.wait_send()


def solution(mesh):
    nx, ny = mesh.shape["gx"], mesh.shape["gy"]
    far = len(far_offsets(nx)) * len(far_offsets(ny)) - 1
    copies = 4 * len(NEAR) + 2 * far
    shapes = []
    for planes, height in zip(PLANES, ROWS):
        shapes += [pltpu.VMEM((planes, height, 128), F32)] * 9

    def per_device(source, inverse_density):
        return pl.pallas_call(
            functools.partial(kernel, nx, ny),
            out_shape=jax.ShapeDtypeStruct(source.shape, F32),
            in_specs=[pl.BlockSpec(memory_space=pl.ANY)] * 2,
            out_specs=pl.BlockSpec(memory_space=pltpu.VMEM),
            scratch_shapes=shapes
            + [
                pltpu.VMEM((20, 48, 128), F32),
                pltpu.VMEM((14, 32, 128), F32),
                pltpu.VMEM((14, 32, 128), F32),
                pltpu.VMEM((25, 2, 8, 128), F32),
                pltpu.VMEM((25, 2, 8, 128), F32),
                pltpu.SemaphoreType.DMA((2,)),
                pltpu.SemaphoreType.DMA((copies,)),
                pltpu.SemaphoreType.DMA((copies,)),
            ],
            compiler_params=pltpu.CompilerParams(collective_id=0, has_side_effects=True),
        )(source, inverse_density)

    placed = (P("gx", "gy", None), P("gx", "gy", None))
    return jax.shard_map(
        per_device, mesh=mesh, in_specs=placed, out_specs=P("gx", "gy", None), check_vma=False
    )
```

```python
import functools

import jax
import jax.numpy as jnp
from jax import lax
from jax.experimental import pallas as pl
from jax.experimental.pallas import tpu as pltpu
from jax.sharding import PartitionSpec as P

MESH = pl.DeviceIdType.MESH
OMEGA = 0.8
F32 = jnp.float32

PLANES = (42, 16, 12, 5)
ROWS = (48, 32, 40, 24)
OWN = 32
NEAR = [(dx, dy) for dx in (1, -1, 0) for dy in (0, 1, -1) if (dx, dy) != (0, 0)]


def far_offsets(peers):
    return (-1, 0, 1, 2) if peers == 4 else (-2, -1, 0, 1, 2)


def lanes(value, shift):
    return pltpu.roll(value, shift % 128, 1)


def rows(value, shift):
    return pltpu.roll(value, shift % value.shape[0], 0)


def lane_index(height):
    return lax.broadcasted_iota(jnp.int32, (height, 128), 1)


def swap_lanes(value, step):
    low = (lane_index(value.shape[0]) & step) == 0
    return jnp.where(low, lanes(value, -step), lanes(value, step))


def loop(first, last, body, unroll=2):
    count = last - first
    whole = count // unroll

    def step(trip, carry):
        for inner in range(unroll):
            body(first + trip * unroll + inner)
        return carry

    lax.fori_loop(0, whole, step, 0)
    for index in range(first + whole * unroll, last):
        body(index)


def bit(number, height):
    return (lane_index(height) & number) != 0


def place_in_group(level, height):
    return lane_index(height) & (2**level - 1)


def next_x(level, here, after):
    if level == 0:
        return after
    size = 2**level
    last = place_in_group(level, here.shape[0]) == size - 1
    return jnp.where(last, lanes(after, size - 1), lanes(here, -1))


def previous_x(level, here, before):
    if level == 0:
        return before
    size = 2**level
    first = place_in_group(level, here.shape[0]) == 0
    return jnp.where(first, lanes(before, 1 - size), lanes(here, 1))


def build(level, b, f, cx, cxm, cy, cz, diag, gain, u):
    height = ROWS[level]
    factor2 = 2.0 * 0.25**level
    step = 2**level
    lane = lane_index(height)
    top = lane >= 128 - step
    ends = top | (lane < step)

    def pair(left, right):
        return factor2 * left * right / (left + right)

    def one(x, carry):
        c_before, here = carry
        after = b[x + 1]
        c_x = pair(here, next_x(level, here, after))
        c_m = previous_x(level, c_x, c_before)
        c_y = pair(here, rows(here, -1))
        c_z = jnp.where(top, 0.0, pair(here, lanes(here, -step)))
        total = c_m + c_x + c_y + rows(c_y, 1) + c_z + lanes(c_z, step)
        total = total + jnp.where(ends, (0.5 * factor2) * here, 0.0)
        scaled = OMEGA / total
        cx[x] = c_x
        if level > 0:
            cxm[x] = c_m
        cy[x] = c_y
        cz[x] = c_z
        diag[x] = total
        gain[x] = scaled
        u[x] = scaled * f[x]
        return (c_x, after)

    first = pair(b[0], next_x(level, b[0], b[1]))
    cx[0] = first
    count = PLANES[level] - 2
    carry = (first, b[1])
    if level == 3:
        for x in range(1, 1 + count):
            carry = one(x, carry)
        return

    def two(trip, carry):
        carry = one(1 + 2 * trip, carry)
        return one(2 + 2 * trip, carry)

    lax.fori_loop(0, count // 2, two, carry)


def spread(level, x, u, cx, cxm, cy, cz, span):
    here = u[x, span]
    along_y = cy[x, span]
    along_z = cz[x, span]
    step = 2**level
    lower = cx[x - 1, span] if level == 0 else cxm[x, span]
    total = cx[x, span] * next_x(level, here, u[x + 1, span])
    total = total + lower * previous_x(level, here, u[x - 1, span])
    total = total + (along_y * rows(here, -1) + rows(along_y * here, 1))
    total = total + (along_z * lanes(here, -step) + lanes(along_z * here, step))
    return here, total


def sweep(level, first, last, source, target, f, cx, cxm, cy, cz, gain, span=None):
    span = pl.ds(0, ROWS[level]) if span is None else span

    def one(x):
        here, total = spread(level, x, source, cx, cxm, cy, cz, span)
        target[x, span] = (1.0 - OMEGA) * here + gain[x, span] * (f[x, span] + total)

    if level == 3:
        for x in range(first, last):
            one(x)
    else:
        loop(first, last, one)


def coarsen(level, values):
    height = values[0].shape[0]
    if level == 0:
        even = ~bit(1, height)
        left, right = values[0] + values[1], values[2] + values[3]
        return jnp.where(even, left, right) + jnp.where(even, lanes(left, -1), lanes(right, 1))
    size = 2**level
    sums = []
    for value in values:
        value = value + swap_lanes(value, 1)
        value = value + swap_lanes(value, size)
        if level == 2:
            value = jnp.where(bit(2, height) == bit(1, height), value, swap_lanes(value, 2))
        sums.append(value)
    low, high = (1, 2) if level == 1 else (2, 4)
    lower = jnp.where(bit(low, height), sums[1], sums[0])
    upper = jnp.where(bit(low, height), sums[3], sums[2])
    return jnp.where(bit(high, height), upper, lower)


def refine(level, value):
    height = value.shape[0]
    if level == 0:
        other = swap_lanes(value, 1)
        low = jnp.where(bit(1, height), other, value)
        high = jnp.where(bit(1, height), value, other)
        return [low, low, high, high]
    outer, inner = (2, 1) if level == 1 else (4, 2)
    other = swap_lanes(value, outer)
    result = []
    for half in (jnp.where(bit(outer, height), other, value), jnp.where(bit(outer, height), value, other)):
        swapped = swap_lanes(half, inner)
        result.append(jnp.where(bit(inner, height), swapped, half))
        result.append(jnp.where(bit(inner, height), half, swapped))
    if level == 2:
        same = bit(2, height) == bit(1, height)
        result = [jnp.where(same, part, swap_lanes(part, 1)) for part in result]
    return result


def pair_rows(tmp, slot, value):
    count = value.shape[0] // 2
    tmp[slot, pl.ds(0, 2 * count)] = value
    summed = tmp[slot, pl.ds(0, count, stride=2)] + tmp[slot, pl.ds(1, count, stride=2)]
    return 0.125 * summed


def restrict(level, plane, target, tmp, fine_x, planes, count, at_x, at_row, limit=None):
    def one(i):
        parts = [fine_x + 4 * i + m for m in range(4)]
        if limit is not None:
            parts = [min(part, limit) for part in parts]
        value = coarsen(level, [plane(part) for part in parts])
        target[at_x + i, pl.ds(at_row, count)] = pair_rows(tmp, i, value)

    if level == 2:
        for i in range(planes):
            one(i)
    else:
        loop(0, planes, one, 1)


def field_plane(b, fine_row, count):
    return lambda x: b[x, pl.ds(fine_row, 2 * count)]


def residual_plane(level, u, f, cx, cxm, cy, cz, diag, fine_row, count):
    span = pl.ds(0, ROWS[level])

    def left(x):
        here, total = spread(level, x, u, cx, cxm, cy, cz, span)
        return (f[x] + total - diag[x] * here)[fine_row : fine_row + 2 * count]

    return left


def add_coarse(level, u, coarse, tmp, first, last, fine_x, coarse_row, fine_row, count, keep=None):
    def one(i):
        trip = i - first
        value = coarse[i, pl.ds(coarse_row, count)]
        tmp[trip, pl.ds(0, count, stride=2)] = value
        tmp[trip, pl.ds(1, count, stride=2)] = value
        span = pl.ds(fine_row, 2 * count)
        for m, part in enumerate(refine(level, tmp[trip, pl.ds(0, 2 * count)])):
            x = fine_x + 4 * trip + m
            if keep is None or x in keep:
                u[x, span] = u[x, span] + part

    if level == 2:
        for i in range(first, last):
            one(i)
    else:
        loop(first, last, one, 1)


def side(offset, length, width, at):
    if offset == 0:
        return pl.ds(0, length), pl.ds(at, length)
    if offset == 1:
        return pl.ds(length - width, width), pl.ds(at - width, width)
    return pl.ds(0, width), pl.ds(at + length, width)


def kernel(nx, ny, f_in, b_in, out, *refs):
    fields = [refs[10 * level : 10 * level + 10] for level in range(4)]
    tmp, load_sem, send_sem, recv_sem = refs[40:]
    (b0, f0, u0, v0, cx0, cm0, cy0, cz0, d0, g0) = fields[0]
    (b1, f1, u1, v1, cx1, cm1, cy1, cz1, d1, g1) = fields[1]
    (b2, f2, u2, v2, cx2, cm2, cy2, cz2, d2, g2) = fields[2]
    (b3, f3, u3, v3, cx3, cm3, cy3, cz3, d3, g3) = fields[3]
    c0, c1, c2, c3 = [(level[4], level[5], level[6], level[7]) for level in fields]
    mx, my = lax.axis_index("gx"), lax.axis_index("gy")
    far = [(dx, dy) for dx in far_offsets(nx) for dy in (-2, -1, 0, 1, 2) if (dx, dy) != (0, 0)]

    def peer(dx, dy):
        return (lax.rem(mx + dx + nx, nx), lax.rem(my + dy + ny, ny))

    barrier = pltpu.get_barrier_semaphore()
    greet = sorted(set(far) | set((-dx, -dy) for dx, dy in far))
    for dx, dy in greet:
        pl.semaphore_signal(barrier, inc=1, device_id=peer(dx, dy), device_id_type=MESH)

    inside = (pl.ds(5, OWN), pl.ds(8, OWN))
    load_b = pltpu.make_async_copy(b_in, b0.at[inside], load_sem.at[0])
    load_f = pltpu.make_async_copy(f_in, f0.at[inside], load_sem.at[1])
    load_b.start()
    load_f.start()
    pl.semaphore_wait(barrier, len(greet))

    started = []

    def send(source, target, dx, dy):
        number = len(started)
        copy = pltpu.make_async_remote_copy(
            src_ref=source,
            dst_ref=target,
            send_sem=send_sem.at[number],
            recv_sem=recv_sem.at[number],
            device_id=peer(dx, dy),
            device_id_type=MESH,
        )
        copy.start()
        started.append(copy)
        return copy

    fine = []
    for dx, dy in NEAR:
        for source, target, width in ((b_in, b0, 5), (f_in, f0, 4)):
            from_x, to_x = side(dx, OWN, width - (dy != 0), 5)
            from_y, to_y = side(dy, OWN, 8, 8)
            fine.append(send(source.at[from_x, from_y], target.at[to_x, to_y], dx, dy))

    def send_1(field):
        copies = []
        for dx, dy in NEAR:
            from_x, to_x = side(dx, 8, 3, 4)
            from_y, to_y = side(dy, 16, 8, 8)
            from_x = pl.ds(from_x.start + 4, from_x.size)
            from_y = pl.ds(from_y.start + 8, from_y.size)
            copies.append(send(field.at[from_x, from_y], field.at[to_x, to_y], dx, dy))
        return copies

    def block_2(field, dx, dy):
        return field.at[pl.ds(5 + 2 * dx, 2), pl.ds(16 + 8 * dy, 8)]

    def send_2(field):
        return [send(block_2(field, 0, 0), block_2(field, -dx, -dy), dx, dy) for dx, dy in far]

    def finish_2(field, copies):
        for copy in copies:
            copy.wait_recv()
        if nx == 4:
            for p in (1, 2):
                field[p + 8] = field[p]

    load_b.wait()
    restrict(0, field_plane(b0, 8, 16), b1, tmp, 5, 8, 16, 4, 8)
    middle_b = send_1(b1)
    restrict(1, field_plane(b1, 8, 8), b2, tmp, 4, 2, 8, 5, 16)
    coarse_b = send_2(b2)
    load_f.wait()
    for copy in fine:
        copy.wait_recv()

    build(0, b0, f0, *c0, d0, g0, u0)
    sweep(0, 2, 40, u0, v0, f0, *c0, g0)
    sweep(0, 3, 39, v0, u0, f0, *c0, g0)
    restrict(0, residual_plane(0, u0, f0, *c0, d0, 8, 16), f1, tmp, 5, 8, 16, 4, 8)
    middle_f = send_1(f1)
    for copy in middle_b:
        copy.wait_recv()
    for copy in middle_f:
        copy.wait_recv()

    build(1, b1, f1, *c1, d1, g1, u1)
    sweep(1, 1, 15, u1, v1, f1, *c1, g1)
    sweep(1, 1, 15, v1, u1, f1, *c1, g1)
    restrict(1, residual_plane(1, u1, f1, *c1, d1, 8, 8), f2, tmp, 4, 2, 8, 5, 16)
    coarse_f = send_2(f2)
    finish_2(b2, coarse_b)
    restrict(2, field_plane(b2, 0, 20), b3, tmp, 1, 3, 20, 1, 0, 10)
    finish_2(f2, coarse_f)

    build(2, b2, f2, *c2, d2, g2, u2)
    sweep(2, 1, 11, u2, v2, f2, *c2, g2)
    sweep(2, 1, 11, v2, u2, f2, *c2, g2)
    restrict(2, residual_plane(2, u2, f2, *c2, d2, 0, 20), f3, tmp, 1, 3, 20, 1, 0, 10)

    build(3, b3, f3, *c3, d3, g3, u3)
    sweep(3, 1, 4, u3, v3, f3, *c3, g3)
    sweep(3, 1, 4, v3, u3, f3, *c3, g3)
    sweep(3, 1, 4, u3, v3, f3, *c3, g3)
    sweep(3, 1, 4, v3, u3, f3, *c3, g3)

    add_coarse(2, u2, u3, tmp, 1, 3, 1, 4, 8, 12, (4, 5, 6, 7))
    middle = pl.ds(8, 24)
    sweep(2, 4, 8, u2, v2, f2, *c2, g2, middle)
    sweep(2, 4, 8, v2, u2, f2, *c2, g2, middle)

    add_coarse(1, u1, u2, tmp, 4, 8, 0, 12, 0, 16)
    sweep(1, 2, 14, u1, v1, f1, *c1, g1)
    sweep(1, 3, 13, v1, u1, f1, *c1, g1)

    add_coarse(0, u0, u1, tmp, 3, 13, 1, 4, 0, 24)
    sweep(0, 4, 38, u0, v0, f0, *c0, g0)

    whole = pl.ds(0, ROWS[0])

    def last(x):
        here, total = spread(0, x, v0, *c0, whole)
        value = (1.0 - OMEGA) * here + g0[x] * (f0[x] + total)
        out[x - 5] = value[8:40]

    loop(5, 37, last)
    for copy in started:
        copy.wait_send()


def solution(mesh):
    nx, ny = mesh.shape["gx"], mesh.shape["gy"]
    far = len(far_offsets(nx)) * 5 - 1
    copies = 4 * len(NEAR) + 2 * far
    shapes = []
    for planes, height in zip(PLANES, ROWS):
        shapes += [pltpu.VMEM((planes, height, 128), F32)] * 10

    def per_device(source, inverse_density):
        return pl.pallas_call(
            functools.partial(kernel, nx, ny),
            out_shape=jax.ShapeDtypeStruct(source.shape, F32),
            in_specs=[pl.BlockSpec(memory_space=pl.ANY)] * 2,
            out_specs=pl.BlockSpec(memory_space=pltpu.VMEM),
            scratch_shapes=shapes
            + [
                pltpu.VMEM((20, 48, 128), F32),
                pltpu.SemaphoreType.DMA((2,)),
                pltpu.SemaphoreType.DMA((copies,)),
                pltpu.SemaphoreType.DMA((copies,)),
            ],
            compiler_params=pltpu.CompilerParams(collective_id=0, has_side_effects=True),
        )(source, inverse_density)

    placed = (P("gx", "gy", None), P("gx", "gy", None))
    return jax.shard_map(
        per_device, mesh=mesh, in_specs=placed, out_specs=P("gx", "gy", None), check_vma=False
    )
```

```python
import functools

import jax
import jax.numpy as jnp
from jax import lax
from jax.experimental import pallas as pl
from jax.experimental.pallas import tpu as pltpu
from jax.sharding import PartitionSpec as P

MESH = pl.DeviceIdType.MESH
OMEGA = 0.8
F32 = jnp.float32

PLANES = (42, 16, 12, 5)
ROWS = (48, 32, 40, 24)
UNROLL = (4, 7, 5, 3)
OWN = 32
NEAR = [(dx, dy) for dx in (1, -1, 0) for dy in (0, 1, -1) if (dx, dy) != (0, 0)]


def far_offsets(peers):
    return (-1, 0, 1, 2) if peers == 4 else (-2, -1, 0, 1, 2)


def lanes(value, shift):
    return pltpu.roll(value, shift % 128, 1)


def rows(value, shift):
    return pltpu.roll(value, shift % value.shape[0], 0)


def lane_index(height):
    return lax.broadcasted_iota(jnp.int32, (height, 128), 1)


def swap_lanes(value, step):
    low = (lane_index(value.shape[0]) & step) == 0
    return jnp.where(low, lanes(value, -step), lanes(value, step))


def loop(first, last, body, unroll=2):
    count = last - first
    whole = count // unroll if count > unroll else 0

    def step(trip, carry):
        for inner in range(unroll):
            body(first + trip * unroll + inner)
        return carry

    if whole:
        lax.fori_loop(0, whole, step, 0)
    for index in range(first + whole * unroll, last):
        body(index)


def bit(number, height):
    return (lane_index(height) & number) != 0


def place_in_group(level, height):
    return lane_index(height) & (2**level - 1)


def next_x(level, here, after):
    if level == 0:
        return after
    size = 2**level
    last = place_in_group(level, here.shape[0]) == size - 1
    return jnp.where(last, lanes(after, size - 1), lanes(here, -1))


def previous_x(level, here, before):
    if level == 0:
        return before
    size = 2**level
    first = place_in_group(level, here.shape[0]) == 0
    return jnp.where(first, lanes(before, 1 - size), lanes(here, 1))


def build(level, first, last, b, cx, cxm, cy, cz, diag, gain, f=None, u=None):
    height = ROWS[level]
    factor2 = 2.0 * 0.25**level
    step = 2**level
    lane = lane_index(height)
    top = lane >= 128 - step
    ends = top | (lane < step)

    def pair(left, right):
        return factor2 * left * right / (left + right)

    def one(x, carry):
        c_before, here = carry
        after = b[x + 1]
        c_x = pair(here, next_x(level, here, after))
        c_m = previous_x(level, c_x, c_before)
        c_y = pair(here, rows(here, -1))
        c_z = jnp.where(top, 0.0, pair(here, lanes(here, -step)))
        total = c_m + c_x + c_y + rows(c_y, 1) + c_z + lanes(c_z, step)
        total = total + jnp.where(ends, (0.5 * factor2) * here, 0.0)
        scaled = OMEGA / total
        cx[x] = c_x
        if level > 0:
            cxm[x] = c_m
        cy[x] = c_y
        cz[x] = c_z
        diag[x] = total
        gain[x] = scaled
        if f is not None:
            u[x] = scaled * f[x]
        return (c_x, after)

    before = pair(b[first - 1], next_x(level, b[first - 1], b[first]))
    cx[first - 1] = before
    count = last - first
    carry = (before, b[first])
    if count < 6:
        for x in range(first, last):
            carry = one(x, carry)
        return

    def two(trip, carry):
        carry = one(first + 2 * trip, carry)
        return one(first + 1 + 2 * trip, carry)

    lax.fori_loop(0, count // 2, two, carry)


def first_sweep(level, first, last, u, f, gain):
    def one(x):
        u[x] = gain[x] * f[x]

    loop(first, last, one, UNROLL[level])


def spread(level, x, u, cx, cxm, cy, cz, span):
    here = u[x, span]
    along_y = cy[x, span]
    along_z = cz[x, span]
    step = 2**level
    lower = cx[x - 1, span] if level == 0 else cxm[x, span]
    total = cx[x, span] * next_x(level, here, u[x + 1, span])
    total = total + lower * previous_x(level, here, u[x - 1, span])
    total = total + (along_y * rows(here, -1) + rows(along_y * here, 1))
    total = total + (along_z * lanes(here, -step) + lanes(along_z * here, step))
    return here, total


def sweep(level, first, last, source, target, f, cx, cxm, cy, cz, gain, span=None):
    span = pl.ds(0, ROWS[level]) if span is None else span

    def one(x):
        here, total = spread(level, x, source, cx, cxm, cy, cz, span)
        target[x, span] = (1.0 - OMEGA) * here + gain[x, span] * (f[x, span] + total)

    loop(first, last, one, UNROLL[level])


def coarsen(level, values):
    height = values[0].shape[0]
    if level == 0:
        even = ~bit(1, height)
        left, right = values[0] + values[1], values[2] + values[3]
        return jnp.where(even, left, right) + jnp.where(even, lanes(left, -1), lanes(right, 1))
    size = 2**level
    sums = []
    for value in values:
        value = value + swap_lanes(value, 1)
        value = value + swap_lanes(value, size)
        if level == 2:
            value = jnp.where(bit(2, height) == bit(1, height), value, swap_lanes(value, 2))
        sums.append(value)
    low, high = (1, 2) if level == 1 else (2, 4)
    lower = jnp.where(bit(low, height), sums[1], sums[0])
    upper = jnp.where(bit(low, height), sums[3], sums[2])
    return jnp.where(bit(high, height), upper, lower)


def refine(level, value):
    height = value.shape[0]
    if level == 0:
        other = swap_lanes(value, 1)
        low = jnp.where(bit(1, height), other, value)
        high = jnp.where(bit(1, height), value, other)
        return [low, low, high, high]
    outer, inner = (2, 1) if level == 1 else (4, 2)
    other = swap_lanes(value, outer)
    result = []
    for half in (jnp.where(bit(outer, height), other, value), jnp.where(bit(outer, height), value, other)):
        swapped = swap_lanes(half, inner)
        result.append(jnp.where(bit(inner, height), swapped, half))
        result.append(jnp.where(bit(inner, height), half, swapped))
    if level == 2:
        same = bit(2, height) == bit(1, height)
        result = [jnp.where(same, part, swap_lanes(part, 1)) for part in result]
    return result


def pair_rows(tmp, slot, value):
    count = value.shape[0] // 2
    tmp[slot, pl.ds(0, 2 * count)] = value
    summed = tmp[slot, pl.ds(0, count, stride=2)] + tmp[slot, pl.ds(1, count, stride=2)]
    return 0.125 * summed


def restrict(level, plane, target, tmp, fine_x, planes, count, at_x, at_row, limit=None):
    def one(i):
        parts = [fine_x + 4 * i + m for m in range(4)]
        if limit is not None:
            parts = [min(part, limit) for part in parts]
        value = coarsen(level, [plane(part) for part in parts])
        target[at_x + i, pl.ds(at_row, count)] = pair_rows(tmp, i, value)

    if level == 2:
        for i in range(planes):
            one(i)
    else:
        loop(0, planes, one, 2)


def field_plane(b, fine_row, count):
    return lambda x: b[x, pl.ds(fine_row, 2 * count)]


def residual_plane(level, u, f, cx, cxm, cy, cz, diag, fine_row, count):
    span = pl.ds(0, ROWS[level])

    def left(x):
        here, total = spread(level, x, u, cx, cxm, cy, cz, span)
        return (f[x] + total - diag[x] * here)[fine_row : fine_row + 2 * count]

    return left


def add_coarse(level, u, coarse, tmp, first, last, fine_x, coarse_row, fine_row, count, keep=None):
    def one(i):
        trip = i - first
        value = coarse[i, pl.ds(coarse_row, count)]
        tmp[trip, pl.ds(0, count, stride=2)] = value
        tmp[trip, pl.ds(1, count, stride=2)] = value
        span = pl.ds(fine_row, 2 * count)
        for m, part in enumerate(refine(level, tmp[trip, pl.ds(0, 2 * count)])):
            x = fine_x + 4 * trip + m
            if keep is None or x in keep:
                u[x, span] = u[x, span] + part

    if level == 2:
        for i in range(first, last):
            one(i)
    else:
        loop(first, last, one, 2)


def side(offset, length, width, at):
    if offset == 0:
        return pl.ds(0, length), pl.ds(at, length)
    if offset == 1:
        return pl.ds(length - width, width), pl.ds(at - width, width)
    return pl.ds(0, width), pl.ds(at + length, width)


def kernel(nx, ny, f_in, b_in, out, *refs):
    fields = [refs[10 * level : 10 * level + 10] for level in range(4)]
    tmp, load_sem, send_sem, recv_sem = refs[40:]
    (b0, f0, u0, v0, cx0, cm0, cy0, cz0, d0, g0) = fields[0]
    (b1, f1, u1, v1, cx1, cm1, cy1, cz1, d1, g1) = fields[1]
    (b2, f2, u2, v2, cx2, cm2, cy2, cz2, d2, g2) = fields[2]
    (b3, f3, u3, v3, cx3, cm3, cy3, cz3, d3, g3) = fields[3]
    c0, c1, c2, c3 = [(level[4], level[5], level[6], level[7]) for level in fields]
    mx, my = lax.axis_index("gx"), lax.axis_index("gy")
    far = [(dx, dy) for dx in far_offsets(nx) for dy in (-2, -1, 0, 1, 2) if (dx, dy) != (0, 0)]

    def peer(dx, dy):
        return (lax.rem(mx + dx + nx, nx), lax.rem(my + dy + ny, ny))

    barrier = pltpu.get_barrier_semaphore()
    greet = sorted(set(far) | set((-dx, -dy) for dx, dy in far))
    for dx, dy in greet:
        pl.semaphore_signal(barrier, inc=1, device_id=peer(dx, dy), device_id_type=MESH)

    inside = (pl.ds(5, OWN), pl.ds(8, OWN))
    load_b = pltpu.make_async_copy(b_in, b0.at[inside], load_sem.at[0])
    load_f = pltpu.make_async_copy(f_in, f0.at[inside], load_sem.at[1])
    load_b.start()
    load_f.start()
    pl.semaphore_wait(barrier, len(greet))

    started = []

    def send(source, target, dx, dy):
        number = len(started)
        copy = pltpu.make_async_remote_copy(
            src_ref=source,
            dst_ref=target,
            send_sem=send_sem.at[number],
            recv_sem=recv_sem.at[number],
            device_id=peer(dx, dy),
            device_id_type=MESH,
        )
        copy.start()
        started.append(copy)
        return copy

    def send_0(dx, dy, wide, skip=0):
        copies = []
        for source, target, width in ((b_in, b0, wide), (f_in, f0, wide - 1)):
            from_x, to_x = side(dx, OWN, width, 5)
            if skip:
                count = 1
                if dx == 1:
                    from_x, to_x = pl.ds(from_x.start, count), pl.ds(to_x.start, count)
                else:
                    from_x = pl.ds(width - 1, count)
                    to_x = pl.ds(5 + OWN + width - 1, count)
            from_y, to_y = side(dy, OWN, 8, 8)
            copies.append(send(source.at[from_x, from_y], target.at[to_x, to_y], dx, dy))
        return copies

    def arrive(copies):
        for copy in copies:
            copy.wait_recv()

    along_y = send_0(0, 1, 5) + send_0(0, -1, 5)
    along_x = send_0(1, 0, 4) + send_0(-1, 0, 4)
    for dx in (1, -1):
        for dy in (1, -1):
            along_x += send_0(dx, dy, 4)

    def send_1(field):
        copies = []
        for dx, dy in NEAR:
            from_x, to_x = side(dx, 8, 3, 4)
            from_y, to_y = side(dy, 16, 8, 8)
            from_x = pl.ds(from_x.start + 4, from_x.size)
            from_y = pl.ds(from_y.start + 8, from_y.size)
            copies.append(send(field.at[from_x, from_y], field.at[to_x, to_y], dx, dy))
        return copies

    def block_2(field, dx, dy):
        return field.at[pl.ds(5 + 2 * dx, 2), pl.ds(16 + 8 * dy, 8)]

    def send_2(field, corners):
        return [
            send(block_2(field, 0, 0), block_2(field, -dx, -dy), dx, dy)
            for dx, dy in far
            if corners or abs(dx) + abs(dy) < 4
        ]

    def finish_2(field, copies):
        for copy in copies:
            copy.wait_recv()
        if nx == 4:
            for p in (1, 2):
                field[p + 8] = field[p]

    load_b.wait()
    restrict(0, field_plane(b0, 8, 16), b1, tmp, 5, 8, 16, 4, 8)
    restrict(1, field_plane(b1, 8, 8), b2, tmp, 4, 2, 8, 5, 16)
    load_f.wait()
    arrive(along_y)
    build(0, 6, 36, b0, *c0, d0, g0, f0, u0)
    sweep(0, 7, 35, u0, v0, f0, *c0, g0)
    arrive(along_x)
    middle_b = send_1(b1)
    outer = []
    for dx in (1, -1):
        outer += send_0(dx, 0, 5, 1)
    build(0, 2, 6, b0, *c0, d0, g0, f0, u0)
    build(0, 36, 40, b0, *c0, d0, g0, f0, u0)
    sweep(0, 3, 7, u0, v0, f0, *c0, g0)
    sweep(0, 35, 39, u0, v0, f0, *c0, g0)
    sweep(0, 4, 38, v0, u0, f0, *c0, g0)
    restrict(0, residual_plane(0, u0, f0, *c0, d0, 8, 16), f1, tmp, 5, 8, 16, 4, 8)
    middle_f = send_1(f1)
    arrive(middle_b)
    build(1, 1, 15, b1, *c1, d1, g1)
    arrive(outer)
    build(0, 1, 2, b0, *c0, d0, g0, f0, u0)
    build(0, 40, 41, b0, *c0, d0, g0, f0, u0)
    for x in (2, 39):
        sweep(0, x, x + 1, u0, v0, f0, *c0, g0)
    for x in (3, 38):
        sweep(0, x, x + 1, v0, u0, f0, *c0, g0)
    arrive(middle_f)
    coarse_b = send_2(b2, True)

    first_sweep(1, 1, 15, u1, f1, g1)
    sweep(1, 1, 15, u1, v1, f1, *c1, g1)
    sweep(1, 1, 15, v1, u1, f1, *c1, g1)
    restrict(1, residual_plane(1, u1, f1, *c1, d1, 8, 8), f2, tmp, 4, 2, 8, 5, 16)
    coarse_f = send_2(f2, False)
    finish_2(b2, coarse_b)
    restrict(2, field_plane(b2, 0, 20), b3, tmp, 1, 3, 20, 1, 0, 10)
    build(2, 1, 11, b2, *c2, d2, g2)
    build(3, 1, 4, b3, *c3, d3, g3)
    finish_2(f2, coarse_f)

    first_sweep(2, 1, 11, u2, f2, g2)
    sweep(2, 1, 11, u2, v2, f2, *c2, g2)
    sweep(2, 1, 11, v2, u2, f2, *c2, g2)
    restrict(2, residual_plane(2, u2, f2, *c2, d2, 0, 20), f3, tmp, 1, 3, 20, 1, 0, 10)

    first_sweep(3, 1, 4, u3, f3, g3)
    sweep(3, 1, 4, u3, v3, f3, *c3, g3)
    sweep(3, 1, 4, v3, u3, f3, *c3, g3)
    sweep(3, 1, 4, u3, v3, f3, *c3, g3)
    sweep(3, 1, 4, v3, u3, f3, *c3, g3)

    add_coarse(2, u2, u3, tmp, 1, 3, 1, 4, 8, 12, (4, 5, 6, 7))
    middle = pl.ds(8, 24)
    sweep(2, 4, 8, u2, v2, f2, *c2, g2, middle)
    sweep(2, 4, 8, v2, u2, f2, *c2, g2, middle)

    add_coarse(1, u1, u2, tmp, 4, 8, 0, 12, 0, 16)
    sweep(1, 2, 14, u1, v1, f1, *c1, g1)
    sweep(1, 3, 13, v1, u1, f1, *c1, g1)

    add_coarse(0, u0, u1, tmp, 3, 13, 1, 4, 0, 24)
    sweep(0, 4, 38, u0, v0, f0, *c0, g0)

    whole = pl.ds(0, ROWS[0])

    def last(x):
        here, total = spread(0, x, v0, *c0, whole)
        value = (1.0 - OMEGA) * here + g0[x] * (f0[x] + total)
        out[x - 5] = value[8:40]

    loop(5, 37, last, 4)
    for copy in started:
        copy.wait_send()


def solution(mesh):
    nx, ny = mesh.shape["gx"], mesh.shape["gy"]
    far = len(far_offsets(nx)) * 5 - 1
    copies = 20 + 2 * len(NEAR) + 2 * far
    shapes = []
    for planes, height in zip(PLANES, ROWS):
        shapes += [pltpu.VMEM((planes, height, 128), F32)] * 10

    def per_device(source, inverse_density):
        return pl.pallas_call(
            functools.partial(kernel, nx, ny),
            out_shape=jax.ShapeDtypeStruct(source.shape, F32),
            in_specs=[pl.BlockSpec(memory_space=pl.ANY)] * 2,
            out_specs=pl.BlockSpec(memory_space=pltpu.VMEM),
            scratch_shapes=shapes
            + [
                pltpu.VMEM((20, 48, 128), F32),
                pltpu.SemaphoreType.DMA((2,)),
                pltpu.SemaphoreType.DMA((copies,)),
                pltpu.SemaphoreType.DMA((copies,)),
            ],
            compiler_params=pltpu.CompilerParams(collective_id=0, has_side_effects=True),
        )(source, inverse_density)

    placed = (P("gx", "gy", None), P("gx", "gy", None))
    return jax.shard_map(
        per_device, mesh=mesh, in_specs=placed, out_specs=P("gx", "gy", None), check_vma=False
    )
```

```python
import functools

import jax
import jax.numpy as jnp
from jax import lax
from jax.experimental import pallas as pl
from jax.experimental.pallas import tpu as pltpu
from jax.sharding import PartitionSpec as P

MESH = pl.DeviceIdType.MESH
OMEGA = 0.8
F32 = jnp.float32

PLANES = (42, 16, 12, 5)
ROWS = (48, 32, 40, 24)
UNROLL = (4, 7, 5, 3)
OWN = 32
NEAR = [(dx, dy) for dx in (1, -1, 0) for dy in (0, 1, -1) if (dx, dy) != (0, 0)]


def far_offsets(peers):
    return (-1, 0, 1, 2) if peers == 4 else (-2, -1, 0, 1, 2)


def lanes(value, shift):
    return pltpu.roll(value, shift % 128, 1)


def rows(value, shift):
    return pltpu.roll(value, shift % value.shape[0], 0)


def lane_index(height):
    return lax.broadcasted_iota(jnp.int32, (height, 128), 1)


def swap_lanes(value, step):
    low = (lane_index(value.shape[0]) & step) == 0
    return jnp.where(low, lanes(value, -step), lanes(value, step))


def loop(first, last, body, unroll=2):
    count = last - first
    whole = count // unroll if count > unroll else 0

    def step(trip, carry):
        for inner in range(unroll):
            body(first + trip * unroll + inner)
        return carry

    if whole:
        lax.fori_loop(0, whole, step, 0)
    for index in range(first + whole * unroll, last):
        body(index)


def bit(number, height):
    return (lane_index(height) & number) != 0


def place_in_group(level, height):
    return lane_index(height) & (2**level - 1)


def next_x(level, here, after):
    if level == 0:
        return after
    size = 2**level
    last = place_in_group(level, here.shape[0]) == size - 1
    return jnp.where(last, lanes(after, size - 1), lanes(here, -1))


def previous_x(level, here, before):
    if level == 0:
        return before
    size = 2**level
    first = place_in_group(level, here.shape[0]) == 0
    return jnp.where(first, lanes(before, 1 - size), lanes(here, 1))


def build(level, first, last, b, cx, cxm, cy, cz, diag, gain, f=None, u=None):
    height = ROWS[level]
    factor2 = 2.0 * 0.25**level
    step = 2**level
    lane = lane_index(height)
    top = lane >= 128 - step
    ends = top | (lane < step)

    def pair(left, right):
        return factor2 * left * right / (left + right)

    def one(x, carry):
        c_before, here = carry
        after = b[x + 1]
        c_x = pair(here, next_x(level, here, after))
        c_m = previous_x(level, c_x, c_before)
        c_y = pair(here, rows(here, -1))
        c_z = jnp.where(top, 0.0, pair(here, lanes(here, -step)))
        total = c_m + c_x + c_y + rows(c_y, 1) + c_z + lanes(c_z, step)
        total = total + jnp.where(ends, (0.5 * factor2) * here, 0.0)
        scaled = OMEGA / total
        cx[x] = c_x
        if level > 0:
            cxm[x] = c_m
        cy[x] = c_y
        cz[x] = c_z
        diag[x] = total
        gain[x] = scaled
        if f is not None:
            u[x] = scaled * f[x]
        return (c_x, after)

    before = pair(b[first - 1], next_x(level, b[first - 1], b[first]))
    cx[first - 1] = before
    count = last - first
    carry = (before, b[first])
    if count < 6:
        for x in range(first, last):
            carry = one(x, carry)
        return

    def two(trip, carry):
        carry = one(first + 2 * trip, carry)
        return one(first + 1 + 2 * trip, carry)

    lax.fori_loop(0, count // 2, two, carry)


def first_sweep(level, first, last, u, f, gain):
    def one(x):
        u[x] = gain[x] * f[x]

    loop(first, last, one, UNROLL[level])


def spread(level, x, u, cx, cxm, cy, cz, span):
    here = u[x, span]
    along_y = cy[x, span]
    along_z = cz[x, span]
    step = 2**level
    lower = cx[x - 1, span] if level == 0 else cxm[x, span]
    total = cx[x, span] * next_x(level, here, u[x + 1, span])
    total = total + lower * previous_x(level, here, u[x - 1, span])
    total = total + (along_y * rows(here, -1) + rows(along_y * here, 1))
    total = total + (along_z * lanes(here, -step) + lanes(along_z * here, step))
    return here, total


def sweep(level, first, last, source, target, f, cx, cxm, cy, cz, gain, span=None):
    span = pl.ds(0, ROWS[level]) if span is None else span

    def one(x):
        here, total = spread(level, x, source, cx, cxm, cy, cz, span)
        target[x, span] = (1.0 - OMEGA) * here + gain[x, span] * (f[x, span] + total)

    loop(first, last, one, UNROLL[level])


def coarsen(level, values):
    height = values[0].shape[0]
    if level == 0:
        even = ~bit(1, height)
        left, right = values[0] + values[1], values[2] + values[3]
        return jnp.where(even, left, right) + jnp.where(even, lanes(left, -1), lanes(right, 1))
    size = 2**level
    sums = []
    for value in values:
        value = value + swap_lanes(value, 1)
        value = value + swap_lanes(value, size)
        if level == 2:
            value = jnp.where(bit(2, height) == bit(1, height), value, swap_lanes(value, 2))
        sums.append(value)
    low, high = (1, 2) if level == 1 else (2, 4)
    lower = jnp.where(bit(low, height), sums[1], sums[0])
    upper = jnp.where(bit(low, height), sums[3], sums[2])
    return jnp.where(bit(high, height), upper, lower)


def refine(level, value):
    height = value.shape[0]
    if level == 0:
        other = swap_lanes(value, 1)
        low = jnp.where(bit(1, height), other, value)
        high = jnp.where(bit(1, height), value, other)
        return [low, low, high, high]
    outer, inner = (2, 1) if level == 1 else (4, 2)
    other = swap_lanes(value, outer)
    result = []
    for half in (jnp.where(bit(outer, height), other, value), jnp.where(bit(outer, height), value, other)):
        swapped = swap_lanes(half, inner)
        result.append(jnp.where(bit(inner, height), swapped, half))
        result.append(jnp.where(bit(inner, height), half, swapped))
    if level == 2:
        same = bit(2, height) == bit(1, height)
        result = [jnp.where(same, part, swap_lanes(part, 1)) for part in result]
    return result


def pair_rows(tmp, slot, value):
    count = value.shape[0] // 2
    tmp[slot, pl.ds(0, 2 * count)] = value
    summed = tmp[slot, pl.ds(0, count, stride=2)] + tmp[slot, pl.ds(1, count, stride=2)]
    return 0.125 * summed


def restrict(level, plane, target, tmp, fine_x, planes, count, at_x, at_row, limit=None):
    def one(i):
        parts = [fine_x + 4 * i + m for m in range(4)]
        if limit is not None:
            parts = [min(part, limit) for part in parts]
        value = coarsen(level, [plane(part) for part in parts])
        target[at_x + i, pl.ds(at_row, count)] = pair_rows(tmp, i, value)

    if level == 2:
        for i in range(planes):
            one(i)
    else:
        loop(0, planes, one, 2)


def field_plane(b, fine_row, count):
    return lambda x: b[x, pl.ds(fine_row, 2 * count)]


def residual_plane(level, u, f, cx, cxm, cy, cz, diag, fine_row, count):
    span = pl.ds(0, ROWS[level])

    def left(x):
        here, total = spread(level, x, u, cx, cxm, cy, cz, span)
        return (f[x] + total - diag[x] * here)[fine_row : fine_row + 2 * count]

    return left


def add_coarse(level, u, coarse, tmp, first, last, fine_x, coarse_row, fine_row, count, keep=None):
    def one(i):
        trip = i - first
        value = coarse[i, pl.ds(coarse_row, count)]
        tmp[trip, pl.ds(0, count, stride=2)] = value
        tmp[trip, pl.ds(1, count, stride=2)] = value
        span = pl.ds(fine_row, 2 * count)
        for m, part in enumerate(refine(level, tmp[trip, pl.ds(0, 2 * count)])):
            x = fine_x + 4 * trip + m
            if keep is None or x in keep:
                u[x, span] = u[x, span] + part

    if level == 2:
        for i in range(first, last):
            one(i)
    else:
        loop(first, last, one, 2)


def side(offset, length, width, at):
    if offset == 0:
        return pl.ds(0, length), pl.ds(at, length)
    if offset == 1:
        return pl.ds(length - width, width), pl.ds(at - width, width)
    return pl.ds(0, width), pl.ds(at + length, width)


def kernel(nx, ny, f_in, b_in, out, *refs):
    fields = [refs[10 * level : 10 * level + 10] for level in range(4)]
    tmp, load_sem, send_sem, recv_sem = refs[40:]
    (b0, f0, u0, v0, cx0, cm0, cy0, cz0, d0, g0) = fields[0]
    (b1, f1, u1, v1, cx1, cm1, cy1, cz1, d1, g1) = fields[1]
    (b2, f2, u2, v2, cx2, cm2, cy2, cz2, d2, g2) = fields[2]
    (b3, f3, u3, v3, cx3, cm3, cy3, cz3, d3, g3) = fields[3]
    c0, c1, c2, c3 = [(level[4], level[5], level[6], level[7]) for level in fields]
    mx, my = lax.axis_index("gx"), lax.axis_index("gy")
    far = [(dx, dy) for dx in far_offsets(nx) for dy in (-2, -1, 0, 1, 2) if (dx, dy) != (0, 0)]

    def peer(dx, dy):
        return (lax.rem(mx + dx + nx, nx), lax.rem(my + dy + ny, ny))

    barrier = pltpu.get_barrier_semaphore()
    for dx, dy in NEAR:
        pl.semaphore_signal(barrier, inc=1, device_id=peer(dx, dy), device_id_type=MESH)

    inside = (pl.ds(5, OWN), pl.ds(8, OWN))
    load_b = pltpu.make_async_copy(b_in, b0.at[inside], load_sem.at[0])
    load_f = pltpu.make_async_copy(f_in, f0.at[inside], load_sem.at[1])
    load_b.start()
    load_f.start()
    pl.semaphore_wait(barrier, len(NEAR))

    started = []

    def send(source, target, dx, dy):
        number = len(started)
        copy = pltpu.make_async_remote_copy(
            src_ref=source,
            dst_ref=target,
            send_sem=send_sem.at[number],
            recv_sem=recv_sem.at[number],
            device_id=peer(dx, dy),
            device_id_type=MESH,
        )
        copy.start()
        started.append(copy)
        return copy

    def send_0(dx, dy, wide, skip=0):
        copies = []
        for source, target, width in ((b_in, b0, wide), (f_in, f0, wide - 1)):
            from_x, to_x = side(dx, OWN, width, 5)
            if skip:
                count = 1
                if dx == 1:
                    from_x, to_x = pl.ds(from_x.start, count), pl.ds(to_x.start, count)
                else:
                    from_x = pl.ds(width - 1, count)
                    to_x = pl.ds(5 + OWN + width - 1, count)
            from_y, to_y = side(dy, OWN, width, 8)
            copies.append(send(source.at[from_x, from_y], target.at[to_x, to_y], dx, dy))
        return copies

    def arrive(copies):
        for copy in copies:
            copy.wait_recv()

    along_y = send_0(0, 1, 5) + send_0(0, -1, 5)
    along_x = send_0(1, 0, 4) + send_0(-1, 0, 4)
    for dx in (1, -1):
        for dy in (1, -1):
            along_x += send_0(dx, dy, 4)

    def send_1(field):
        copies = []
        for dx, dy in NEAR:
            from_x, to_x = side(dx, 8, 3, 4)
            from_y, to_y = side(dy, 16, 8, 8)
            from_x = pl.ds(from_x.start + 4, from_x.size)
            from_y = pl.ds(from_y.start + 8, from_y.size)
            copies.append(send(field.at[from_x, from_y], field.at[to_x, to_y], dx, dy))
        return copies

    def block_2(field, dx, dy):
        return field.at[pl.ds(5 + 2 * dx, 2), pl.ds(16 + 8 * dy, 8)]

    def send_2(field, corners):
        return [
            send(block_2(field, 0, 0), block_2(field, -dx, -dy), dx, dy)
            for dx, dy in far
            if corners or abs(dx) + abs(dy) < 4
        ]

    def finish_2(field, copies):
        for copy in copies:
            copy.wait_recv()
        if nx == 4:
            for p in (1, 2):
                field[p + 8] = field[p]

    load_b.wait()
    restrict(0, field_plane(b0, 8, 16), b1, tmp, 5, 8, 16, 4, 8)
    restrict(1, field_plane(b1, 8, 8), b2, tmp, 4, 2, 8, 5, 16)
    load_f.wait()
    arrive(along_y)
    build(0, 6, 36, b0, *c0, d0, g0, f0, u0)
    sweep(0, 7, 35, u0, v0, f0, *c0, g0)
    arrive(along_x)
    middle_b = send_1(b1)
    outer = []
    for dx in (1, -1):
        outer += send_0(dx, 0, 5, 1)
    coarse_b = send_2(b2, True)
    build(0, 2, 6, b0, *c0, d0, g0, f0, u0)
    build(0, 36, 40, b0, *c0, d0, g0, f0, u0)
    sweep(0, 3, 7, u0, v0, f0, *c0, g0)
    sweep(0, 35, 39, u0, v0, f0, *c0, g0)
    sweep(0, 4, 38, v0, u0, f0, *c0, g0)
    restrict(0, residual_plane(0, u0, f0, *c0, d0, 8, 16), f1, tmp, 5, 8, 16, 4, 8)
    middle_f = send_1(f1)
    arrive(middle_b)
    build(1, 1, 15, b1, *c1, d1, g1)
    arrive(outer)
    build(0, 1, 2, b0, *c0, d0, g0, f0, u0)
    build(0, 40, 41, b0, *c0, d0, g0, f0, u0)
    for x in (2, 39):
        sweep(0, x, x + 1, u0, v0, f0, *c0, g0)
    for x in (3, 38):
        sweep(0, x, x + 1, v0, u0, f0, *c0, g0)
    arrive(middle_f)

    first_sweep(1, 1, 15, u1, f1, g1)
    sweep(1, 1, 15, u1, v1, f1, *c1, g1)
    sweep(1, 1, 15, v1, u1, f1, *c1, g1)
    restrict(1, residual_plane(1, u1, f1, *c1, d1, 8, 8), f2, tmp, 4, 2, 8, 5, 16)
    coarse_f = send_2(f2, False)
    finish_2(b2, coarse_b)
    restrict(2, field_plane(b2, 0, 20), b3, tmp, 1, 3, 20, 1, 0, 10)
    build(2, 1, 11, b2, *c2, d2, g2)
    build(3, 1, 4, b3, *c3, d3, g3)
    finish_2(f2, coarse_f)

    first_sweep(2, 1, 11, u2, f2, g2)
    sweep(2, 1, 11, u2, v2, f2, *c2, g2)
    sweep(2, 1, 11, v2, u2, f2, *c2, g2)
    restrict(2, residual_plane(2, u2, f2, *c2, d2, 0, 20), f3, tmp, 1, 3, 20, 1, 0, 10)

    first_sweep(3, 1, 4, u3, f3, g3)
    sweep(3, 1, 4, u3, v3, f3, *c3, g3)
    sweep(3, 1, 4, v3, u3, f3, *c3, g3)
    sweep(3, 1, 4, u3, v3, f3, *c3, g3)
    sweep(3, 1, 4, v3, u3, f3, *c3, g3)

    add_coarse(2, u2, u3, tmp, 1, 3, 1, 4, 8, 12, (4, 5, 6, 7))
    middle = pl.ds(8, 24)
    sweep(2, 4, 8, u2, v2, f2, *c2, g2, middle)
    sweep(2, 4, 8, v2, u2, f2, *c2, g2, middle)

    add_coarse(1, u1, u2, tmp, 4, 8, 0, 12, 0, 16)
    sweep(1, 2, 14, u1, v1, f1, *c1, g1)
    sweep(1, 3, 13, v1, u1, f1, *c1, g1)

    add_coarse(0, u0, u1, tmp, 3, 13, 1, 4, 0, 24)
    sweep(0, 4, 38, u0, v0, f0, *c0, g0)

    whole = pl.ds(0, ROWS[0])

    def last(x):
        here, total = spread(0, x, v0, *c0, whole)
        value = (1.0 - OMEGA) * here + g0[x] * (f0[x] + total)
        out[x - 5] = value[8:40]

    loop(5, 37, last, 4)
    for copy in started:
        copy.wait_send()


def solution(mesh):
    nx, ny = mesh.shape["gx"], mesh.shape["gy"]
    far = len(far_offsets(nx)) * 5 - 1
    copies = 20 + 2 * len(NEAR) + 2 * far
    shapes = []
    for planes, height in zip(PLANES, ROWS):
        shapes += [pltpu.VMEM((planes, height, 128), F32)] * 10

    def per_device(source, inverse_density):
        return pl.pallas_call(
            functools.partial(kernel, nx, ny),
            out_shape=jax.ShapeDtypeStruct(source.shape, F32),
            in_specs=[pl.BlockSpec(memory_space=pl.ANY)] * 2,
            out_specs=pl.BlockSpec(memory_space=pltpu.VMEM),
            scratch_shapes=shapes
            + [
                pltpu.VMEM((20, 48, 128), F32),
                pltpu.SemaphoreType.DMA((2,)),
                pltpu.SemaphoreType.DMA((copies,)),
                pltpu.SemaphoreType.DMA((copies,)),
            ],
            compiler_params=pltpu.CompilerParams(collective_id=0, has_side_effects=True),
        )(source, inverse_density)

    placed = (P("gx", "gy", None), P("gx", "gy", None))
    return jax.shard_map(
        per_device, mesh=mesh, in_specs=placed, out_specs=P("gx", "gy", None), check_vma=False
    )
```
